256 devices in a mesh: section: 8 (over x, core), seq: 32 (over z, y).
Axes of the slice: x: 4, y: 4, z: 8, core: 2. Of those that a mesh axis runs over, the one named last changes fastest.
Arguments:
- activations: bfloat16 [8, 8192, 1536], P('section', 'seq'), may hold values from -6 to 6
- qkv_weight: bfloat16 [8, 1536, 4608], P('section'), may hold values from -5 to 5
- out_weight: bfloat16 [8, 1536, 1536], P('section'), may hold values from -0.15625 to 0.15625
- modulation: float32 [8, 3, 1536], P('section'), may hold values from -4 to 4
- key_blocks: int32 [64, 4], replicated, may hold values from 0 to 63, as said below
- block_counts: int32 [64], replicated, may hold values from 3 to 4, as said below
Outputs:
- advanced: bfloat16 [8, 8192, 1536], P('section', 'seq')
The draws below stay inside these ranges and needn't reach their ends.
Inputs may be any that keep to these rules, and one draw needn't show every extreme that they name: Block b belongs to group b // 2. Row b of key_blocks names first its own block, then the other blocks of its group, then 2 blocks of different groups g with 1 <= |g - b // 2| <= 2. All rows of one group name at most one block of any other group. `block_counts`: some query block uses all 4 entries.
All inputs are finite; a program needn't handle non-finite values.
Results may differ from the reference program's by a relative error of at most 0.008.
Values may be sent and summed in bfloat16 or wider, within the bound.
A program may use at most 128 MiB of HBM per device.

```python
import jax
import jax.numpy as jnp
from jax import lax

D = 1536
HEADS = 12
HD = 128
BLK = 128
REMOTE = 2
SECTIONS = 8
TOKENS = 8192
BLK_DEV = 2
NBLK = 64
NSEL = 4


def draw_activations(key, part):
    base = jnp.clip(jax.random.normal(key, (SECTIONS, TOKENS, D), jnp.float32), -5.0, 5.0)
    return base.astype(jnp.bfloat16)


def draw_qkv_weight(key, part):
    inner_width = HEADS * HD
    base = jnp.clip(jax.random.normal(key, (SECTIONS, D, 3 * inner_width), jnp.float32), -4.0, 4.0) * D ** (-0.5)
    return base.astype(jnp.bfloat16)


def draw_key_blocks(key, part):
    seq_count = NBLK // BLK_DEV
    aligned = jax.random.randint(jax.random.fold_in(key, 11), (seq_count, seq_count), 0, BLK_DEV)
    block_index = jnp.arange(NBLK, dtype=jnp.int32)
    device_of = block_index // BLK_DEV
    local_of = block_index % BLK_DEV
    own_part = device_of[:, None] * BLK_DEV + (local_of[:, None] + jnp.arange(BLK_DEV, dtype=jnp.int32)[None, :]) % BLK_DEV
    candidates = jnp.array([-2, -1, 1, 2], dtype=jnp.int32)
    targets = device_of[:, None] + candidates[None, :]
    valid = (targets >= 0) & (targets < seq_count)
    ranking = jax.random.randint(jax.random.fold_in(key, 12), (NBLK, 4), 0, 1 << 20)
    ranking = ranking * 4 + jnp.arange(4, dtype=jnp.int32)[None, :] + jnp.where(valid, 0, 1 << 24)
    ordering = jnp.argsort(ranking, axis=1)[:, :REMOTE]
    offsets = jnp.take_along_axis(jnp.broadcast_to(candidates[None, :], (NBLK, 4)), ordering, axis=1)
    peers = device_of[:, None] + offsets
    far_part = peers * BLK_DEV + aligned[device_of[:, None], peers]
    return jnp.concatenate([own_part, far_part], axis=1).astype(jnp.int32)


def draw_block_counts(key, part):
    counts_drawn = jax.random.randint(jax.random.fold_in(key, 21), (NBLK,), BLK_DEV + 1, NSEL + 1)
    filled_spot = jax.random.randint(jax.random.fold_in(key, 22), (), 0, NBLK)
    return jnp.where(jnp.arange(NBLK, dtype=jnp.int32) == filled_spot, NSEL, counts_drawn).astype(jnp.int32)


def block_scale(key, shape, cuts, smallest, largest):
    level = 1.0
    for axis_at, parts in cuts:
        heights = jax.random.uniform(jax.random.fold_in(jax.random.fold_in(key, 6), axis_at), (parts,), jnp.float32, smallest / len(cuts), largest / len(cuts))
        level = level * jnp.repeat(jnp.exp(heights), shape[axis_at] // parts).reshape((-1,) + (1,) * (len(shape) - 1 - axis_at))
    return level


def noise(own_key, extent, deviation, most, shards=(), kind=jnp.bfloat16):
    drawn = jax.random.normal(own_key, extent, jnp.float32) * deviation
    if len(shards) > 0:
        drawn = block_scale(own_key, extent, shards, -0.22, 0.18) * drawn
    return jnp.clip(drawn, min=-most, max=most).astype(kind)


def setup_inputs(seed: int = 0) -> dict:
    keys = jax.random.split(jax.random.key(seed), 7)
    return {
        "activations": draw_activations(jax.random.fold_in(keys[6], 71), 0),
        "qkv_weight": draw_qkv_weight(jax.random.fold_in(keys[6], 71), 0),
        "out_weight": noise(keys[2], (SECTIONS, HEADS * HD, D), (HEADS * HD) ** -0.5, 0.15625, ((0, 8),)),
        "modulation": noise(keys[3], (SECTIONS, 3, D), 1.0, 4.0, ((0, 8),), jnp.float32),
        "key_blocks": draw_key_blocks(jax.random.fold_in(keys[6], 71), 0),
        "block_counts": draw_block_counts(jax.random.fold_in(keys[6], 71), 0),
    }


EPSILON = 1e-06

def modulated_norm(tokens_in, segment_mod):
    values = tokens_in.astype(jnp.float32)
    center = lax.optimization_barrier(jnp.mean(values, axis=-1, keepdims=True))
    spread = lax.optimization_barrier(jnp.mean(jnp.square(values - center), axis=-1, keepdims=True))
    normed = (values - center) * lax.rsqrt(spread + EPSILON)
    return (normed * (1.0 + segment_mod[1]) + segment_mod[0]).astype(jnp.bfloat16)

def segment_layer(tokens_in, weights_in, weights_out, segment_mod, key_blocks, block_counts):
    token_count = tokens_in.shape[0]
    inner_width = HEADS * HD
    block_total = token_count // BLK
    list_width = key_blocks.shape[1]
    modulated = modulated_norm(tokens_in, segment_mod)
    projected = jnp.dot(modulated, weights_in, preferred_element_type=jnp.float32).astype(jnp.bfloat16)
    query_blocks = projected[:, :inner_width].reshape(block_total, BLK, HEADS, HD)
    pair_blocks = projected[:, inner_width:].reshape(block_total, BLK, 2 * inner_width)

    def one_block(operands):
        query_block, row, count = operands
        picked = jnp.take(pair_blocks, row, axis=0).reshape(list_width * BLK, 2 * inner_width)
        key_part = picked[:, :inner_width].reshape(list_width * BLK, HEADS, HD).astype(jnp.float32)
        value_part = picked[:, inner_width:].reshape(list_width * BLK, HEADS, HD)
        scores = jnp.einsum('qhd,khd->hqk', query_block.astype(jnp.float32), key_part) * HD ** (-0.5)
        live = jnp.repeat(jnp.arange(list_width, dtype=jnp.int32) < count, BLK)
        scores = jnp.where(live[None, None, :], scores, -jnp.inf)
        row_peak = lax.optimization_barrier(jnp.max(scores, axis=-1, keepdims=True))
        exponent = jnp.exp(scores - row_peak)
        denominator = lax.optimization_barrier(jnp.sum(exponent, axis=-1, keepdims=True))
        weighted = jnp.einsum('hqk,khd->hqd', exponent.astype(jnp.bfloat16).astype(jnp.float32), value_part.astype(jnp.float32))
        return jnp.moveaxis(weighted / denominator, 0, 1)
    attended = lax.map(one_block, (query_blocks, key_blocks, block_counts))
    attended = attended.reshape(token_count, inner_width).astype(jnp.bfloat16)
    output = jnp.dot(attended, weights_out, preferred_element_type=jnp.float32)
    return (tokens_in.astype(jnp.float32) + segment_mod[2] * output).astype(jnp.bfloat16)

def reference(activations, qkv_weight, out_weight, modulation, key_blocks, block_counts):

    def advance_segment(operands):
        return segment_layer(operands[0], operands[1], operands[2], operands[3], key_blocks, block_counts)
    first_pass = lax.map(advance_segment, (activations, qkv_weight, out_weight, modulation))
    handed_over = jnp.roll(first_pass, 1, axis=0)
    return lax.map(advance_segment, (handed_over, qkv_weight, out_weight, modulation))
```

```python
import functools

import jax
import jax.numpy as jnp
from jax import lax
from jax.experimental import pallas as pl
from jax.experimental.pallas import tpu as pltpu
from jax.sharding import PartitionSpec as P

MESH = pl.DeviceIdType.MESH

D = 1536
HEADS = 12
HD = 128
BLK = 128
EPSILON = 1e-06
NEG = -1e30
SCALE = HD**-0.5 * 1.4426950408889634

CH = 4
ROWS = BLK // CH
TN = 512


def kernel(
    sections,
    seqs,
    kb,
    cnt,
    x_hbm,
    wqkv_hbm,
    wout_hbm,
    mod,
    out_ref,
    xbuf,
    x1,
    xin,
    snd,
    rcv,
    wqkv,
    wout,
    mn,
    mh,
    qb,
    kvo,
    kvh,
    acc,
    mst,
    lst,
    att,
    sem_in,
    send_sem,
    recv_sem,
    shift_send,
    shift_recv,
):
    s = lax.axis_index("section")
    g = lax.axis_index("seq")
    up, down = lax.rem(g + 1, seqs), lax.rem(g + seqs - 1, seqs)
    nxt, prv = lax.rem(s + 1, sections), lax.rem(s + sections - 1, sections)

    x_in = pltpu.make_async_copy(x_hbm, xbuf, sem_in.at[0])
    x_in.start()
    w_in = []
    for j in range(3):
        cols = pl.ds(j * D, D)
        w_in.append(
            pltpu.make_async_copy(wqkv_hbm.at[:, cols], wqkv.at[:, cols], sem_in.at[1 + j])
        )
    w_in.append(pltpu.make_async_copy(wout_hbm, wout, sem_in.at[4]))
    for cp in w_in:
        cp.start()

    barrier = pltpu.get_barrier_semaphore()
    for dev in ((s, up), (s, down), (nxt, g), (prv, g)):
        pl.semaphore_signal(barrier, inc=1, device_id=dev, device_id_type=MESH)

    def wanted(d):
        target = lax.rem(g + d + seqs, seqs)
        pick = jnp.int32(0)
        for r in range(2):
            row = target * 2 + r
            for j in (2, 3):
                entry = kb[row, j]
                live = jnp.logical_and(entry // 2 == g, j < cnt[row])
                pick = jnp.where(live, entry % 2, pick)
        return pick

    picks = [wanted(d) for d in (1, -1, 2, -2)]

    def bias_of(r, d):
        row = g * 2 + r
        hit = jnp.bool_(False)
        for j in (2, 3):
            hit = jnp.logical_or(
                hit, jnp.logical_and(kb[row, j] // 2 == g + d, j < cnt[row])
            )
        return jnp.where(hit, jnp.float32(0.0), jnp.float32(NEG))

    bias = {d: [bias_of(r, d) for r in range(2)] for d in (-1, 1, -2, 2)}

    def flow(l, f, c):
        rows = pl.ds(c * ROWS, ROWS)
        src = snd.at[l, f, rows] if f < 4 else rcv.at[l, f - 2, rows]
        return pltpu.make_async_remote_copy(
            src_ref=src,
            dst_ref=rcv.at[l, f, rows],
            send_sem=send_sem.at[l, f, c],
            recv_sem=recv_sem.at[l, f, c],
            device_id=(s, up if f % 2 == 0 else down),
            device_id_type=MESH,
        )

    def shift(c):
        rows = pl.ds(c * ROWS, ROWS)
        return pltpu.make_async_remote_copy(
            src_ref=x1.at[:, rows],
            dst_ref=xin.at[:, rows],
            send_sem=shift_send.at[c],
            recv_sem=shift_recv.at[c],
            device_id=(nxt, g),
            device_id_type=MESH,
        )

    def normed(v):
        v = v.astype(jnp.float32)
        center = jnp.mean(v, axis=-1, keepdims=True)
        v = v - center
        spread = jnp.mean(jnp.square(v), axis=-1, keepdims=True)
        v = v * lax.rsqrt(spread + EPSILON)
        return (v * (1.0 + mod[1:2, :]) + mod[0:1, :]).astype(jnp.bfloat16)

    NR = 64

    def norm_own(src):
        for r in range(2):

            def body(i, carry):
                rows = pl.ds(pl.multiple_of(i * NR, NR), NR)
                mn[r, rows] = normed(src[r, rows])
                return carry

            lax.fori_loop(0, BLK // NR, body, 0)

    def project(src, w_first, tiles, dst, dst_first, rows_of):
        def body(j, carry):
            wcol = pl.multiple_of(w_first + j * TN, TN)
            dcol = pl.multiple_of(dst_first + j * TN, TN)
            y = jnp.dot(
                src, wqkv[:, pl.ds(wcol, TN)], preferred_element_type=jnp.float32
            ).astype(jnp.bfloat16)
            rows_of(dst, pl.ds(dcol, TN), y)
            return carry

        lax.fori_loop(0, tiles, body, 0)

    def attend(keys, first, last, biases):
        def body(h, carry):
            cols = pl.ds(pl.multiple_of(h * HD, HD), HD)
            vcols = pl.ds(pl.multiple_of(D + h * HD, HD), HD)
            kh = keys(cols)
            vh = keys(vcols)
            for r in range(2):
                qh = qb[r, :, cols]
                sc = lax.dot_general(
                    qh, kh, (((1,), (1,)), ((), ())), preferred_element_type=jnp.float32
                )
                s0 = sc[:, :BLK] * SCALE
                s1 = sc[:, BLK:] * SCALE
                if biases is not None:
                    s0 = s0 + biases[0][r]
                    s1 = s1 + biases[1][r]
                peak = jnp.max(jnp.maximum(s0, s1), axis=-1, keepdims=True)
                if first:
                    mnew = jnp.broadcast_to(peak, (BLK, HD))
                else:
                    mold = mst[h, r]
                    mnew = jnp.maximum(mold, peak)
                p0 = jnp.exp2(s0 - mnew)
                p1 = jnp.exp2(s1 - mnew)
                total = jnp.sum(p0 + p1, axis=-1, keepdims=True)
                p = jnp.concatenate([p0, p1], axis=1).astype(jnp.bfloat16)
                pv = jnp.dot(p, vh, preferred_element_type=jnp.float32)
                if first:
                    lnew = jnp.broadcast_to(total, (BLK, HD))
                else:
                    alpha = jnp.exp2(mold - mnew)
                    lnew = lst[h, r] * alpha + total
                    pv = acc[r, :, cols] * alpha + pv
                if last:
                    att[r, :, cols] = (pv / lnew).astype(jnp.bfloat16)
                else:
                    acc[r, :, cols] = pv
                    mst[h, r] = mnew
                    lst[h, r] = lnew
            return carry

        lax.fori_loop(0, HEADS, body, 0)

    def select(l, src, c):
        rows = pl.ds(c * ROWS, ROWS)
        lower, upper = src[0, rows], src[1, rows]
        for f in range(4):
            snd[l, f, rows] = jnp.where(picks[f] == 0, lower, upper)

    def layer(l, src, emit):
        norm_own(src)
        if l == 0:
            for cp in w_in[:3]:
                cp.wait()

        def put_own(dst, cols, y):
            dst[:, :, cols] = y.reshape(2, BLK, TN)

        own = mn[...].reshape(2 * BLK, D)
        project(own, 0, D // TN, qb, 0, put_own)
        project(own, D, 2 * D // TN, kvo, 0, put_own)
        attend(lambda cols: kvo[:, :, cols].reshape(2 * BLK, HD), True, False, None)

        for c in range(CH):
            for f in (0, 1):
                flow(l, f, c).wait_recv()
        for f in (0, 1):

            def near(i, carry):
                rows = pl.ds(pl.multiple_of(i * NR, NR), NR)
                mh[f, rows] = normed(rcv[l, f, rows])
                return carry

            lax.fori_loop(0, BLK // NR, near, 0)

        def put_near(dst, cols, y):
            dst[0, :, :, cols] = y.reshape(2, BLK, TN)

        project(mh[...].reshape(2 * BLK, D), D, 2 * D // TN, kvh, 0, put_near)
        for c in range(CH // 2):
            for f in (2, 3):
                flow(l, f, c).wait_recv()
                flow(l, f + 2, c).start()
        attend(
            lambda cols: kvh[0, :, :, cols].reshape(2 * BLK, HD),
            False,
            False,
            (bias[-1], bias[1]),
        )
        for c in range(CH // 2, CH):
            for f in (2, 3):
                flow(l, f, c).wait_recv()
                flow(l, f + 2, c).start()

        half = BLK // 2
        for i in range(2):
            rows = pl.ds(i * half, half)
            for c in range(i * CH // 2, (i + 1) * CH // 2):
                for f in (4, 5):
                    flow(l, f, c).wait_recv()
            for f in (4, 5):
                mh[f - 4, rows] = normed(rcv[l, f, rows])

            def put_far(dst, cols, y):
                dst[1, :, rows, cols] = y.reshape(2, half, TN)

            project(mh[:, rows].reshape(2 * half, D), D, 2 * D // TN, kvh, 0, put_far)
        attend(
            lambda cols: kvh[1, :, :, cols].reshape(2 * BLK, HD),
            False,
            True,
            (bias[-2], bias[2]),
        )

        if l == 0:
            w_in[3].wait()
        for i in range(2):
            rows = pl.ds(i * half, half)
            a = att[:, rows].reshape(2 * half, D)
            for j in range(D // TN):
                cols = pl.ds(j * TN, TN)
                y = jnp.dot(a, wout[:, cols], preferred_element_type=jnp.float32)
                res = src[:, rows, cols].astype(jnp.float32).reshape(2 * half, TN)
                res = res + mod[2:3, cols] * y
                emit(rows, cols, res.astype(jnp.bfloat16).reshape(2, half, TN))
            if l == 0:
                for c in range(i * CH // 2, (i + 1) * CH // 2):
                    shift(c).start()

    x_in.wait()
    for c in range(CH):
        select(0, xbuf, c)
    pl.semaphore_wait(barrier, 4)
    for fs in ((0, 1), (2, 3)):
        for c in range(CH):
            for f in fs:
                flow(0, f, c).start()

    def emit_first(rows, cols, y):
        x1[:, rows, cols] = y

    layer(0, xbuf, emit_first)

    for c in range(CH):
        shift(c).wait_recv()
        select(1, xin, c)
        for f in (0, 1):
            flow(1, f, c).start()
    for c in range(CH):
        for f in (2, 3):
            flow(1, f, c).start()

    def emit_second(rows, cols, y):
        out_ref[:, rows, cols] = y

    layer(1, xin, emit_second)

    for c in range(CH):
        shift(c).wait_send()
        for l in range(2):
            for f in range(6):
                flow(l, f, c).wait_send()


def on_device(sections, seqs, activations, qkv_weight, out_weight, modulation, key_blocks, block_counts):
    bf16, f32 = jnp.bfloat16, jnp.float32
    dma = pltpu.SemaphoreType.DMA
    out = pl.pallas_call(
        functools.partial(kernel, sections, seqs),
        out_shape=jax.ShapeDtypeStruct((2, BLK, D), bf16),
        in_specs=[
            pl.BlockSpec(memory_space=pltpu.SMEM),
            pl.BlockSpec(memory_space=pltpu.SMEM),
            pl.BlockSpec(memory_space=pl.ANY),
            pl.BlockSpec(memory_space=pl.ANY),
            pl.BlockSpec(memory_space=pl.ANY),
            pl.BlockSpec(memory_space=pltpu.VMEM),
        ],
        out_specs=pl.BlockSpec(memory_space=pltpu.VMEM),
        scratch_shapes=[
            pltpu.VMEM((2, BLK, D), bf16),
            pltpu.VMEM((2, BLK, D), bf16),
            pltpu.VMEM((2, BLK, D), bf16),
            pltpu.VMEM((2, 4, BLK, D), bf16),
            pltpu.VMEM((2, 6, BLK, D), bf16),
            pltpu.VMEM((D, 3 * D), bf16),
            pltpu.VMEM((D, D), bf16),
            pltpu.VMEM((2, BLK, D), bf16),
            pltpu.VMEM((2, BLK, D), bf16),
            pltpu.VMEM((2, BLK, D), bf16),
            pltpu.VMEM((2, BLK, 2 * D), bf16),
            pltpu.VMEM((2, 2, BLK, 2 * D), bf16),
            pltpu.VMEM((2, BLK, D), f32),
            pltpu.VMEM((HEADS, 2, BLK, HD), f32),
            pltpu.VMEM((HEADS, 2, BLK, HD), f32),
            pltpu.VMEM((2, BLK, D), bf16),
            dma((5,)),
            dma((2, 6, CH)),
            dma((2, 6, CH)),
            dma((CH,)),
            dma((CH,)),
        ],
        compiler_params=pltpu.CompilerParams(
            collective_id=0, has_side_effects=True, vmem_limit_bytes=60 * 1024 * 1024
        ),
        name="two_layers",
    )(
        key_blocks,
        block_counts,
        activations.reshape(2, BLK, D),
        qkv_weight[0],
        out_weight[0],
        modulation[0],
    )
    return out.reshape(1, 2 * BLK, D)


def solution(mesh):
    return jax.shard_map(
        functools.partial(on_device, mesh.shape["section"], mesh.shape["seq"]),
        mesh=mesh,
        in_specs=(
            P("section", "seq", None),
            P("section", None, None),
            P("section", None, None),
            P("section", None, None),
            P(),
            P(),
        ),
        out_specs=P("section", "seq", None),
        check_vma=False,
    )
```

```python
import functools

import jax
import jax.numpy as jnp
from jax import lax
from jax.experimental import pallas as pl
from jax.experimental.pallas import tpu as pltpu
from jax.sharding import PartitionSpec as P

MESH = pl.DeviceIdType.MESH

D = 1536
HEADS = 12
HD = 128
BLK = 128
EPSILON = 1e-06
NEG = -1e30
SCALE = HD**-0.5 * 1.4426950408889634

CH = 4
SH = 8
TN = 512
UH = 4


def kernel(
    sections,
    seqs,
    kb,
    cnt,
    x_hbm,
    wqkv_hbm,
    wout_hbm,
    mod,
    out_ref,
    xbuf,
    x1,
    xin,
    snd,
    rcv,
    wqkv,
    wout,
    mown,
    qkv,
    kvn,
    kvf,
    acc,
    mst,
    lst,
    att,
    sem_in,
    send_sem,
    recv_sem,
    shift_send,
    shift_recv,
):
    s = lax.axis_index("section")
    g = lax.axis_index("seq")
    up, down = lax.rem(g + 1, seqs), lax.rem(g + seqs - 1, seqs)
    nxt, prv = lax.rem(s + 1, sections), lax.rem(s + sections - 1, sections)

    x_in = pltpu.make_async_copy(x_hbm, xbuf, sem_in.at[0])
    x_in.start()
    w_in = []
    for j in range(3):
        cols = pl.ds(j * D, D)
        w_in.append(
            pltpu.make_async_copy(wqkv_hbm.at[:, cols], wqkv.at[:, cols], sem_in.at[1 + j])
        )
    w_in.append(pltpu.make_async_copy(wout_hbm, wout, sem_in.at[4]))
    for cp in w_in:
        cp.start()

    barrier = pltpu.get_barrier_semaphore()
    for dev in ((s, up), (s, down), (nxt, g), (prv, g)):
        pl.semaphore_signal(barrier, inc=1, device_id=dev, device_id_type=MESH)

    def wanted(d):
        target = lax.rem(g + d + seqs, seqs)
        pick = jnp.int32(0)
        for r in range(2):
            row = target * 2 + r
            for j in (2, 3):
                entry = kb[j, row]
                live = jnp.logical_and(entry // 2 == g, j < cnt[row])
                pick = jnp.where(live, entry % 2, pick)
        return pick

    picks = [wanted(d) for d in (1, -1, 2, -2)]

    def bias_of(r, d):
        row = g * 2 + r
        hit = jnp.bool_(False)
        for j in (2, 3):
            hit = jnp.logical_or(
                hit, jnp.logical_and(kb[j, row] // 2 == g + d, j < cnt[row])
            )
        return jnp.where(hit, jnp.float32(0.0), jnp.float32(NEG))

    bias = {d: [bias_of(r, d) for r in range(2)] for d in (-1, 1, -2, 2)}
    lane = lax.broadcasted_iota(jnp.int32, (1, HD), 1)
    far = [jnp.where(lane < BLK // 2, bias[-2][r], bias[2][r]) for r in range(2)]

    def flow(l, f, c, n):
        rows = pl.ds(c * (BLK // n), BLK // n)
        src = snd.at[l, f, rows] if f < 4 else rcv.at[l, f - 2, rows]
        return pltpu.make_async_remote_copy(
            src_ref=src,
            dst_ref=rcv.at[l, f, rows],
            send_sem=send_sem.at[l, f, c],
            recv_sem=recv_sem.at[l, f, c],
            device_id=(s, up if f % 2 == 0 else down),
            device_id_type=MESH,
        )

    def shift(c):
        rows = pl.ds(c * (BLK // SH), BLK // SH)
        return pltpu.make_async_remote_copy(
            src_ref=x1.at[:, rows],
            dst_ref=xin.at[:, rows],
            send_sem=shift_send.at[c],
            recv_sem=shift_recv.at[c],
            device_id=(nxt, g),
            device_id_type=MESH,
        )

    def normed(v):
        v = v.astype(jnp.float32)
        center = jnp.mean(v, axis=-1, keepdims=True)
        v = v - center
        spread = jnp.mean(jnp.square(v), axis=-1, keepdims=True)
        v = v * lax.rsqrt(spread + EPSILON)
        return (v * (1.0 + mod[1]) + mod[0]).astype(jnp.bfloat16)

    def select(l, fs, rows):
        lower, upper = mown[0, rows], mown[1, rows]
        for f in fs:
            snd[l, f, rows] = jnp.where(picks[f] == 0, lower, upper)

    def project(src, w_first, steps, dst):
        def body(j, carry):
            for t in range(D // TN):
                wcol = pl.multiple_of(w_first + j * D + t * TN, TN)
                dcol = pl.multiple_of(j * D + t * TN, TN)
                y = jnp.dot(
                    src(), wqkv[:, pl.ds(wcol, TN)], preferred_element_type=jnp.float32
                )
                dst(pl.ds(dcol, TN), y.astype(jnp.bfloat16))
            return carry

        lax.fori_loop(0, steps, body, 0)

    def attend(keys, first, last):
        def body(i, carry):
            at = []
            for u in range(UH):
                h = i * UH + u
                at.append(pl.ds(pl.multiple_of(h * HD, HD), HD))
            scores, old, new, done = {}, {}, {}, {}
            for u in range(UH):
                h = i * UH + u
                qh = qkv[:, :, at[u]].reshape(2 * BLK, HD)
                if not first:
                    old[u] = (mst[h], lst[h], acc[:, :, at[u]].reshape(2 * BLK, HD))
                parts = []
                for load, masks in keys:
                    sc = lax.dot_general(
                        qh,
                        load(h, 0),
                        (((1,), (1,)), ((), ())),
                        preferred_element_type=jnp.float32,
                    )
                    for k in range(sc.shape[1] // HD):
                        part = sc[:, k * HD : (k + 1) * HD] * SCALE
                        if masks is not None:
                            part = jnp.concatenate(
                                [part[:BLK] + masks[k][0], part[BLK:] + masks[k][1]], axis=0
                            )
                        parts.append(part)
                scores[u] = parts
            for u in range(UH):
                peak = scores[u][0]
                for part in scores[u][1:]:
                    peak = jnp.maximum(peak, part)
                peak = jnp.max(peak, axis=-1, keepdims=True)
                if first:
                    new[u] = jnp.broadcast_to(peak, (2 * BLK, HD))
                else:
                    new[u] = jnp.maximum(old[u][0], peak)
            for u in range(UH):
                ps = [jnp.exp2(part - new[u]) for part in scores[u]]
                total = ps[0]
                for p in ps[1:]:
                    total = total + p
                total = jnp.sum(total, axis=-1, keepdims=True)
                pv, k = None, 0
                for load, _ in keys:
                    v = load(i * UH + u, 1)
                    n = v.shape[0] // HD
                    p = ps[k] if n == 1 else jnp.concatenate(ps[k : k + n], axis=1)
                    k += n
                    y = jnp.dot(
                        p.astype(jnp.bfloat16), v, preferred_element_type=jnp.float32
                    )
                    pv = y if pv is None else pv + y
                if first:
                    total = jnp.broadcast_to(total, (2 * BLK, HD))
                else:
                    alpha = jnp.exp2(old[u][0] - new[u])
                    total = old[u][1] * alpha + total
                    pv = old[u][2] * alpha + pv
                done[u] = (total, pv)
            for u in range(UH):
                total, pv = done[u]
                if last:
                    y = (pv / total).astype(jnp.bfloat16)
                    att[:, :, at[u]] = y.reshape(2, BLK, HD)
                else:
                    h = i * UH + u
                    mst[h] = new[u]
                    lst[h] = total
                    acc[:, :, at[u]] = pv.reshape(2, BLK, HD)
            return carry

        lax.fori_loop(0, HEADS // UH, body, 0)

    def cols_of(h, which, base):
        return pl.ds(pl.multiple_of(base + which * D + h * HD, HD), HD)

    def own_keys(h, which):
        return qkv[:, :, cols_of(h, which, D)].reshape(2 * BLK, HD)

    def near_keys(h, which):
        return kvn[:, :, cols_of(h, which, 0)].reshape(2 * BLK, HD)

    def far_keys(i):
        return lambda h, which: kvf[i, :, cols_of(h, which, 0)]

    def layer(l, src, emit):
        n = CH if l == 0 else SH
        if l == 0:
            x_in.wait()
        for c in range(n):
            rows = pl.ds(c * (BLK // n), BLK // n)
            if l == 1:
                shift(c).wait_recv()
            for r in range(2):
                mown[r, rows] = normed(src[r, rows])
            select(l, (0, 1), rows)
            if l == 0 and c == 0:
                pl.semaphore_wait(barrier, 4)
            for f in (0, 1):
                flow(l, f, c, n).start()
        select(l, (2, 3), pl.ds(0, BLK))
        for c in range(CH):
            for f in (2, 3):
                flow(l, f, c, CH).start()

        if l == 0:
            for cp in w_in[:3]:
                cp.wait()

        def put_own(cols, y):
            qkv[:, :, cols] = y.reshape(2, BLK, TN)

        project(lambda: mown[...].reshape(2 * BLK, D), 0, 3, put_own)

        for c in range(n):
            for f in (0, 1):
                flow(l, f, c, n).wait_recv()

        def put_near(cols, y):
            kvn[:, :, cols] = y.reshape(2, BLK, TN)

        project(lambda: rcv[l, 0:2].reshape(2 * BLK, D), D, 2, put_near)
        for c in range(CH):
            for f in (2, 3):
                flow(l, f, c, CH).wait_recv()
                flow(l, f + 2, c, CH).start()
        attend(
            [(own_keys, None), (near_keys, (bias[-1], bias[1]))],
            True,
            False,
        )

        half = BLK // 2
        for i in range(2):
            rows = pl.ds(i * half, half)
            for c in range(i * CH // 2, (i + 1) * CH // 2):
                for f in (4, 5):
                    flow(l, f, c, CH).wait_recv()

            def put_far(cols, y):
                kvf[i, :, cols] = y

            project(lambda: rcv[l, 4:6, rows].reshape(2 * half, D), D, 2, put_far)
            attend([(far_keys(i), (far,))], False, i == 1)

        if l == 0:
            w_in[3].wait()
        for j in range(D // TN):
            cols = pl.ds(j * TN, TN)
            y = jnp.dot(
                att[...].reshape(2 * BLK, D),
                wout[:, cols],
                preferred_element_type=jnp.float32,
            )
            res = src[:, :, cols].astype(jnp.float32).reshape(2 * BLK, TN)
            res = res + mod[2, :, cols] * y
            emit(cols, res.astype(jnp.bfloat16).reshape(2, BLK, TN))

    def emit_first(cols, y):
        x1[:, :, cols] = y

    def emit_second(cols, y):
        out_ref[:, :, cols] = y

    layer(0, xbuf, emit_first)
    for c in range(SH):
        shift(c).start()
    layer(1, xin, emit_second)

    for c in range(SH):
        shift(c).wait_send()
    for l in range(2):
        for f in range(6):
            n = SH if l == 1 and f < 2 else CH
            for c in range(n):
                flow(l, f, c, n).wait_send()


def on_device(sections, seqs, activations, qkv_weight, out_weight, modulation, key_blocks, block_counts):
    bf16, f32 = jnp.bfloat16, jnp.float32
    dma = pltpu.SemaphoreType.DMA
    out = pl.pallas_call(
        functools.partial(kernel, sections, seqs),
        out_shape=jax.ShapeDtypeStruct((2, BLK, D), bf16),
        in_specs=[
            pl.BlockSpec(memory_space=pltpu.SMEM),
            pl.BlockSpec(memory_space=pltpu.SMEM),
            pl.BlockSpec(memory_space=pltpu.HBM),
            pl.BlockSpec(memory_space=pltpu.HBM),
            pl.BlockSpec(memory_space=pltpu.HBM),
            pl.BlockSpec(memory_space=pltpu.VMEM),
        ],
        out_specs=pl.BlockSpec(memory_space=pltpu.VMEM),
        scratch_shapes=[
            pltpu.VMEM((2, BLK, D), bf16),
            pltpu.VMEM((2, BLK, D), bf16),
            pltpu.VMEM((2, BLK, D), bf16),
            pltpu.VMEM((2, 4, BLK, D), bf16),
            pltpu.VMEM((2, 6, BLK, D), bf16),
            pltpu.VMEM((D, 3 * D), bf16),
            pltpu.VMEM((D, D), bf16),
            pltpu.VMEM((2, BLK, D), bf16),
            pltpu.VMEM((2, BLK, 3 * D), bf16),
            pltpu.VMEM((2, BLK, 2 * D), bf16),
            pltpu.VMEM((2, BLK, 2 * D), bf16),
            pltpu.VMEM((2, BLK, D), f32),
            pltpu.VMEM((HEADS, 2 * BLK, HD), f32),
            pltpu.VMEM((HEADS, 2 * BLK, HD), f32),
            pltpu.VMEM((2, BLK, D), bf16),
            dma((5,)),
            dma((2, 6, SH)),
            dma((2, 6, SH)),
            dma((SH,)),
            dma((SH,)),
        ],
        compiler_params=pltpu.CompilerParams(
            collective_id=0, has_side_effects=True, vmem_limit_bytes=60 * 1024 * 1024
        ),
        name="two_layers",
    )(
        key_blocks.T,
        block_counts,
        activations.reshape(2, BLK, D),
        qkv_weight[0],
        out_weight[0],
        modulation.transpose(1, 0, 2),
    )
    return out.reshape(1, 2 * BLK, D)


def solution(mesh):
    return jax.shard_map(
        functools.partial(on_device, mesh.shape["section"], mesh.shape["seq"]),
        mesh=mesh,
        in_specs=(
            P("section", "seq", None),
            P("section", None, None),
            P("section", None, None),
            P("section", None, None),
            P(),
            P(),
        ),
        out_specs=P("section", "seq", None),
        check_vma=False,
    )
```

```python
import functools

import jax
import jax.numpy as jnp
from jax import lax
from jax.experimental import pallas as pl
from jax.experimental.pallas import tpu as pltpu
from jax.sharding import PartitionSpec as P

MESH = pl.DeviceIdType.MESH

D = 1536
HEADS = 12
HD = 128
BLK = 128
EPSILON = 1e-06
NEG = -1e30
SCALE = HD**-0.5 * 1.4426950408889634

CH = 4
SH = 8
TN = 512
UH = 4


def aligned(first):
    return first if isinstance(first, int) else pl.multiple_of(first, HD)


def kernel(
    sections,
    seqs,
    kb,
    cnt,
    x_hbm,
    wqkv_hbm,
    wout_hbm,
    mod,
    out_ref,
    xbuf,
    x1,
    xin,
    snd,
    rcv,
    wqkv,
    wout,
    mown,
    qkv,
    kvn,
    kvf,
    acc,
    mst,
    lst,
    att,
    sem_in,
    send_sem,
    recv_sem,
    shift_send,
    shift_recv,
):
    s = lax.axis_index("section")
    g = lax.axis_index("seq")
    up, down = lax.rem(g + 1, seqs), lax.rem(g + seqs - 1, seqs)
    nxt, prv = lax.rem(s + 1, sections), lax.rem(s + sections - 1, sections)

    x_in = pltpu.make_async_copy(x_hbm, xbuf, sem_in.at[0])
    x_in.start()
    w_in = []
    for j in range(3):
        cols = pl.ds(j * D, D)
        w_in.append(
            pltpu.make_async_copy(wqkv_hbm.at[:, cols], wqkv.at[:, cols], sem_in.at[1 + j])
        )
    w_in.append(pltpu.make_async_copy(wout_hbm, wout, sem_in.at[4]))
    for cp in w_in:
        cp.start()

    def sends(f):
        reach = 1 if f < 2 else 2
        if f < 4:
            return g + reach < seqs if f % 2 == 0 else g >= reach
        return interior

    def receives(f):
        if f < 2:
            return g >= 1 if f == 0 else g + 1 < seqs
        if f < 4:
            return interior
        return g >= 2 if f == 4 else g + 2 < seqs

    has_up, has_down = g + 1 < seqs, g >= 1
    interior = jnp.logical_and(has_up, has_down)

    barrier = pltpu.get_barrier_semaphore()
    for dev in ((nxt, g), (prv, g)):
        pl.semaphore_signal(barrier, inc=1, device_id=dev, device_id_type=MESH)
    for dev, there in (((s, up), has_up), ((s, down), has_down)):

        @pl.when(there)
        def _():
            pl.semaphore_signal(barrier, inc=1, device_id=dev, device_id_type=MESH)

    for f in (0, 1, 4, 5):

        @pl.when(jnp.logical_not(receives(f)))
        def _():
            for l in range(2):
                rcv[l, f] = jnp.zeros((BLK, D), jnp.bfloat16)

    def wanted(d):
        target = lax.rem(g + d + seqs, seqs)
        pick = jnp.int32(0)
        for r in range(2):
            row = target * 2 + r
            for j in (2, 3):
                entry = kb[j, row]
                live = jnp.logical_and(entry // 2 == g, j < cnt[row])
                pick = jnp.where(live, entry % 2, pick)
        return pick

    picks = [wanted(d) for d in (1, -1, 2, -2)]

    def bias_of(r, d):
        row = g * 2 + r
        hit = jnp.bool_(False)
        for j in (2, 3):
            hit = jnp.logical_or(
                hit, jnp.logical_and(kb[j, row] // 2 == g + d, j < cnt[row])
            )
        return jnp.where(hit, jnp.float32(0.0), jnp.float32(NEG))

    bias = {d: [bias_of(r, d) for r in range(2)] for d in (-1, 1, -2, 2)}
    lane = lax.broadcasted_iota(jnp.int32, (1, HD), 1)
    far = [jnp.where(lane < BLK // 2, bias[-2][r], bias[2][r]) for r in range(2)]

    def flow(l, f, c, n):
        rows = pl.ds(c * (BLK // n), BLK // n)
        src = snd.at[l, f, rows] if f < 4 else rcv.at[l, f - 2, rows]
        return pltpu.make_async_remote_copy(
            src_ref=src,
            dst_ref=rcv.at[l, f, rows],
            send_sem=send_sem.at[l, f, c],
            recv_sem=recv_sem.at[l, f, c],
            device_id=(s, up if f % 2 == 0 else down),
            device_id_type=MESH,
        )

    def shift(c):
        rows = pl.ds(c * (BLK // SH), BLK // SH)
        return pltpu.make_async_remote_copy(
            src_ref=x1.at[:, rows],
            dst_ref=xin.at[:, rows],
            send_sem=shift_send.at[c],
            recv_sem=shift_recv.at[c],
            device_id=(nxt, g),
            device_id_type=MESH,
        )

    def normed(v):
        v = v.astype(jnp.float32)
        center = jnp.mean(v, axis=-1, keepdims=True)
        v = v - center
        spread = jnp.mean(jnp.square(v), axis=-1, keepdims=True)
        v = v * lax.rsqrt(spread + EPSILON)
        return (v * (1.0 + mod[1]) + mod[0]).astype(jnp.bfloat16)

    def select(l, fs, rows):
        lower, upper = mown[0, rows], mown[1, rows]
        for f in fs:
            snd[l, f, rows] = jnp.where(picks[f] == 0, lower, upper)

    def project(src, w_first, steps, dst, scaled=False):
        def body(j, carry):
            for t in range(D // TN):
                wcol = pl.multiple_of(w_first + j * D + t * TN, TN)
                dcol = pl.multiple_of(j * D + t * TN, TN)
                y = jnp.dot(
                    src(), wqkv[:, pl.ds(wcol, TN)], preferred_element_type=jnp.float32
                )
                if scaled:
                    y = y * jnp.where(j == 0, jnp.float32(SCALE), jnp.float32(1.0))
                dst(pl.ds(dcol, TN), y.astype(jnp.bfloat16))
            return carry

        lax.fori_loop(0, steps, body, 0)

    def heads(i, keys, first, last):
        at = []
        for u in range(UH):
            h = i * UH + u
            at.append(pl.ds(aligned(h * HD), HD))
        scores, old, new, done = {}, {}, {}, {}
        for u in range(UH):
            h = i * UH + u
            qh = qkv[:, :, at[u]].reshape(2 * BLK, HD)
            if not first:
                old[u] = (mst[h], lst[h], acc[:, :, at[u]].reshape(2 * BLK, HD))
            parts = []
            for load, masks in keys:
                sc = lax.dot_general(
                    qh,
                    load(h, 0),
                    (((1,), (1,)), ((), ())),
                    preferred_element_type=jnp.float32,
                )
                for k in range(sc.shape[1] // HD):
                    part = sc[:, k * HD : (k + 1) * HD]
                    if masks is not None:
                        part = jnp.concatenate(
                            [part[:BLK] + masks[k][0], part[BLK:] + masks[k][1]], axis=0
                        )
                    parts.append(part)
            scores[u] = parts
        for u in range(UH):
            peak = scores[u][0]
            for part in scores[u][1:]:
                peak = jnp.maximum(peak, part)
            peak = jnp.max(peak, axis=-1, keepdims=True)
            if first:
                new[u] = jnp.broadcast_to(peak, (2 * BLK, HD))
            else:
                new[u] = jnp.maximum(old[u][0], peak)
        for u in range(UH):
            ps = [jnp.exp2(part - new[u]) for part in scores[u]]
            pv, k = None, 0
            for load, _ in keys:
                v = load(i * UH + u, 1)
                n = v.shape[0] // HD
                p = ps[k] if n == 1 else jnp.concatenate(ps[k : k + n], axis=1)
                k += n
                v = jnp.concatenate([v, jnp.ones_like(v)], axis=1)
                y = jnp.dot(
                    p.astype(jnp.bfloat16), v, preferred_element_type=jnp.float32
                )
                pv = y if pv is None else pv + y
            pv, total = pv[:, :HD], pv[:, HD:]
            if not first:
                alpha = jnp.exp2(old[u][0] - new[u])
                total = old[u][1] * alpha + total
                pv = old[u][2] * alpha + pv
            done[u] = (total, pv)
        for u in range(UH):
            total, pv = done[u]
            if last:
                y = (pv / total).astype(jnp.bfloat16)
                att[:, :, at[u]] = y.reshape(2, BLK, HD)
            else:
                h = i * UH + u
                mst[h] = new[u]
                lst[h] = total
                acc[:, :, at[u]] = pv.reshape(2, BLK, HD)

    def attend(keys, first, last, before=None):
        def body(i, carry):
            if before is not None:
                before(i)
            heads(i, keys, first, last)
            return carry

        lax.fori_loop(0, HEADS // UH, body, 0)

    def cols_of(h, which, base):
        return pl.ds(aligned(base + which * D + h * HD), HD)

    def own_keys(h, which):
        return qkv[:, :, cols_of(h, which, D)].reshape(2 * BLK, HD)

    def near_keys(h, which):
        return kvn[:, :, cols_of(h, which, 0)].reshape(2 * BLK, HD)

    def far_keys(i):
        return lambda h, which: kvf[i, :, cols_of(h, which, 0)]

    def layer(l, src, emit):
        n = CH if l == 0 else SH
        if l == 0:
            x_in.wait()
        for c in range(n):
            rows = pl.ds(c * (BLK // n), BLK // n)
            if l == 1:
                shift(c).wait_recv()
            for r in range(2):
                mown[r, rows] = normed(src[r, rows])
            select(l, (0, 1), rows)
            if l == 0 and c == 0:
                peers = 2 + has_up.astype(jnp.int32) + has_down.astype(jnp.int32)
                pl.semaphore_wait(barrier, peers)
            for f in (0, 1):

                @pl.when(sends(f))
                def _():
                    flow(l, f, c, n).start()

        select(l, (2, 3), pl.ds(0, BLK))
        for f in (2, 3):

            @pl.when(sends(f))
            def _():
                for c in range(CH):
                    flow(l, f, c, CH).start()


        if l == 0:
            for cp in w_in[:3]:
                cp.wait()

        def put_own(cols, y):
            qkv[:, :, cols] = y.reshape(2, BLK, TN)

        project(lambda: mown[...].reshape(2 * BLK, D), 0, 3, put_own, True)

        for f in (0, 1):

            @pl.when(receives(f))
            def _():
                for c in range(n):
                    flow(l, f, c, n).wait_recv()

        def put_near(cols, y):
            kvn[:, :, cols] = y.reshape(2, BLK, TN)

        project(lambda: rcv[l, 0:2].reshape(2 * BLK, D), D, 2, put_near)


        def relay(c):
            @pl.when(interior)
            def _():
                for f in (2, 3):
                    flow(l, f, c, CH).wait_recv()
                    flow(l, f + 2, c, CH).start()

        attend([(own_keys, None), (near_keys, (bias[-1], bias[1]))], True, False, relay)
        for c in range(HEADS // UH, CH):
            relay(c)

        half = BLK // 2
        for i in range(2):
            rows = pl.ds(i * half, half)
            for f in (4, 5):

                @pl.when(receives(f))
                def _():
                    for c in range(i * CH // 2, (i + 1) * CH // 2):
                        flow(l, f, c, CH).wait_recv()

            groups = HEADS // UH
            wide = UH * HD
            for j in range(groups + 1):
                if j < groups:
                    for first in (j * wide, D + j * wide):
                        y = jnp.dot(
                            rcv[l, 4:6, rows].reshape(2 * half, D),
                            wqkv[:, pl.ds(D + first, wide)],
                            preferred_element_type=jnp.float32,
                        )
                        kvf[i, :, pl.ds(first, wide)] = y.astype(jnp.bfloat16)
                if j >= 1:
                    heads(j - 1, [(far_keys(i), (far,))], False, i == 1)

        if l == 0:
            w_in[3].wait()
        for j in range(D // TN):
            cols = pl.ds(j * TN, TN)
            y = jnp.dot(
                att[...].reshape(2 * BLK, D),
                wout[:, cols],
                preferred_element_type=jnp.float32,
            )
            res = src[:, :, cols].astype(jnp.float32).reshape(2 * BLK, TN)
            res = res + mod[2, :, cols] * y
            emit(cols, res.astype(jnp.bfloat16).reshape(2, BLK, TN))

    def emit_first(cols, y):
        x1[:, :, cols] = y

    def emit_second(cols, y):
        out_ref[:, :, cols] = y

    layer(0, xbuf, emit_first)
    for c in range(SH):
        shift(c).start()
    layer(1, xin, emit_second)

    for c in range(SH):
        shift(c).wait_send()
    for f in range(6):

        @pl.when(sends(f))
        def _():
            for l in range(2):
                n = SH if l == 1 and f < 2 else CH
                for c in range(n):
                    flow(l, f, c, n).wait_send()


def on_device(sections, seqs, activations, qkv_weight, out_weight, modulation, key_blocks, block_counts):
    bf16, f32 = jnp.bfloat16, jnp.float32
    dma = pltpu.SemaphoreType.DMA
    out = pl.pallas_call(
        functools.partial(kernel, sections, seqs),
        out_shape=pltpu.VMEM((2, BLK, D), bf16),
        in_specs=[
            pl.BlockSpec(memory_space=pltpu.SMEM),
            pl.BlockSpec(memory_space=pltpu.SMEM),
            pl.BlockSpec(memory_space=pltpu.HBM),
            pl.BlockSpec(memory_space=pltpu.HBM),
            pl.BlockSpec(memory_space=pltpu.HBM),
            pl.BlockSpec(memory_space=pltpu.VMEM),
        ],
        out_specs=pl.BlockSpec(memory_space=pltpu.VMEM),
        scratch_shapes=[
            pltpu.VMEM((2, BLK, D), bf16),
            pltpu.VMEM((2, BLK, D), bf16),
            pltpu.VMEM((2, BLK, D), bf16),
            pltpu.VMEM((2, 4, BLK, D), bf16),
            pltpu.VMEM((2, 6, BLK, D), bf16),
            pltpu.VMEM((D, 3 * D), bf16),
            pltpu.VMEM((D, D), bf16),
            pltpu.VMEM((2, BLK, D), bf16),
            pltpu.VMEM((2, BLK, 3 * D), bf16),
            pltpu.VMEM((2, BLK, 2 * D), bf16),
            pltpu.VMEM((2, BLK, 2 * D), bf16),
            pltpu.VMEM((2, BLK, D), f32),
            pltpu.VMEM((HEADS, 2 * BLK, HD), f32),
            pltpu.VMEM((HEADS, 2 * BLK, HD), f32),
            pltpu.VMEM((2, BLK, D), bf16),
            dma((5,)),
            dma((2, 6, SH)),
            dma((2, 6, SH)),
            dma((SH,)),
            dma((SH,)),
        ],
        compiler_params=pltpu.CompilerParams(
            collective_id=0, has_side_effects=True, vmem_limit_bytes=62 * 1024 * 1024
        ),
        name="two_layers",
    )(
        key_blocks.T,
        block_counts,
        activations.reshape(2, BLK, D),
        qkv_weight[0],
        out_weight[0],
        modulation.transpose(1, 0, 2),
    )
    return out.reshape(1, 2 * BLK, D)


def solution(mesh):
    return jax.shard_map(
        functools.partial(on_device, mesh.shape["section"], mesh.shape["seq"]),
        mesh=mesh,
        in_specs=(
            P("section", "seq", None),
            P("section", None, None),
            P("section", None, None),
            P("section", None, None),
            P(),
            P(),
        ),
        out_specs=P("section", "seq", None),
        check_vma=False,
    )
```

```python
import functools

import jax
import jax.numpy as jnp
from jax import lax
from jax.experimental import pallas as pl
from jax.experimental.pallas import tpu as pltpu
from jax.sharding import PartitionSpec as P

MESH = pl.DeviceIdType.MESH

D = 1536
HEADS = 12
HD = 128
BLK = 128
EPSILON = 1e-06
NEG = -1e30
SCALE = HD**-0.5 * 1.4426950408889634

CH = 4
SH = 8
TN = 512
UH = 4


def aligned(first):
    return first if isinstance(first, int) else pl.multiple_of(first, HD)


def kernel(
    sections,
    seqs,
    kb,
    cnt,
    x_hbm,
    wqkv_hbm,
    wout_hbm,
    mod,
    out_ref,
    xbuf,
    x1,
    xin,
    snd,
    rcv,
    wqkv,
    wout,
    mown,
    qkv,
    kvn,
    kvf,
    acc,
    mst,
    lst,
    att,
    sem_in,
    send_sem,
    recv_sem,
    shift_send,
    shift_recv,
):
    s = lax.axis_index("section")
    g = lax.axis_index("seq")
    up, down = lax.rem(g + 1, seqs), lax.rem(g + seqs - 1, seqs)
    nxt, prv = lax.rem(s + 1, sections), lax.rem(s + sections - 1, sections)

    x_in = []
    for j, rows in enumerate((pl.ds(0, BLK // CH), pl.ds(BLK // CH, BLK - BLK // CH))):
        x_in.append(
            pltpu.make_async_copy(x_hbm.at[:, rows], xbuf.at[:, rows], sem_in.at[5 * j])
        )
    for cp in x_in:
        cp.start()
    w_in = []
    for j in range(3):
        cols = pl.ds(j * D, D)
        w_in.append(
            pltpu.make_async_copy(wqkv_hbm.at[:, cols], wqkv.at[:, cols], sem_in.at[1 + j])
        )
    w_in.append(pltpu.make_async_copy(wout_hbm, wout, sem_in.at[4]))
    for cp in w_in:
        cp.start()

    def sends(f):
        reach = 1 if f < 2 else 2
        if f < 4:
            return g + reach < seqs if f % 2 == 0 else g >= reach
        return interior

    def receives(f):
        if f < 2:
            return g >= 1 if f == 0 else g + 1 < seqs
        if f < 4:
            return interior
        return g >= 2 if f == 4 else g + 2 < seqs

    has_up, has_down = g + 1 < seqs, g >= 1
    interior = jnp.logical_and(has_up, has_down)

    barrier = pltpu.get_barrier_semaphore()
    for dev in ((nxt, g), (prv, g)):
        pl.semaphore_signal(barrier, inc=1, device_id=dev, device_id_type=MESH)
    for dev, there in (((s, up), has_up), ((s, down), has_down)):

        @pl.when(there)
        def _():
            pl.semaphore_signal(barrier, inc=1, device_id=dev, device_id_type=MESH)

    def wanted(d):
        target = lax.rem(g + d + seqs, seqs)
        pick = jnp.int32(0)
        for r in range(2):
            row = target * 2 + r
            for j in (2, 3):
                entry = kb[j, row]
                live = jnp.logical_and(entry // 2 == g, j < cnt[row])
                pick = jnp.where(live, entry % 2, pick)
        return pick

    picks = [wanted(d) for d in (1, -1, 2, -2)]

    def bias_of(r, d):
        row = g * 2 + r
        hit = jnp.bool_(False)
        for j in (2, 3):
            hit = jnp.logical_or(
                hit, jnp.logical_and(kb[j, row] // 2 == g + d, j < cnt[row])
            )
        return jnp.where(hit, jnp.float32(0.0), jnp.float32(NEG))

    bias, far = {}, []

    def flow(l, f, c, n):
        rows = pl.ds(c * (BLK // n), BLK // n)
        src = snd.at[l, f, rows] if f < 4 else rcv.at[l, f - 2, rows]
        return pltpu.make_async_remote_copy(
            src_ref=src,
            dst_ref=rcv.at[l, f, rows],
            send_sem=send_sem.at[l, f, c],
            recv_sem=recv_sem.at[l, f, c],
            device_id=(s, up if f % 2 == 0 else down),
            device_id_type=MESH,
        )

    def shift(c):
        rows = pl.ds(c * (BLK // SH), BLK // SH)
        return pltpu.make_async_remote_copy(
            src_ref=x1.at[:, rows],
            dst_ref=xin.at[:, rows],
            send_sem=shift_send.at[c],
            recv_sem=shift_recv.at[c],
            device_id=(nxt, g),
            device_id_type=MESH,
        )

    def normed(v):
        v = v.astype(jnp.float32)
        center = jnp.mean(v, axis=-1, keepdims=True)
        v = v - center
        spread = jnp.mean(jnp.square(v), axis=-1, keepdims=True)
        v = v * lax.rsqrt(spread + EPSILON)
        return (v * (1.0 + mod[1]) + mod[0]).astype(jnp.bfloat16)

    def select(l, fs, rows):
        lower, upper = mown[0, rows], mown[1, rows]
        for f in fs:
            snd[l, f, rows] = jnp.where(picks[f] == 0, lower, upper)

    def project(src, w_first, steps, dst, scaled=False):
        def body(j, carry):
            for t in range(D // TN):
                wcol = pl.multiple_of(w_first + j * D + t * TN, TN)
                dcol = pl.multiple_of(j * D + t * TN, TN)
                y = jnp.dot(
                    src(), wqkv[:, pl.ds(wcol, TN)], preferred_element_type=jnp.float32
                )
                if scaled:
                    y = y * jnp.where(j == 0, jnp.float32(SCALE), jnp.float32(1.0))
                dst(pl.ds(dcol, TN), y.astype(jnp.bfloat16))
            return carry

        lax.fori_loop(0, steps, body, 0)

    def heads(i, keys, first, last, beside=()):
        at = []
        for u in range(UH):
            h = i * UH + u
            at.append(pl.ds(aligned(h * HD), HD))
        scores, old, new, done = {}, {}, {}, {}
        for u in range(UH):
            h = i * UH + u
            qh = qkv[:, :, at[u]].reshape(2 * BLK, HD)
            if not first:
                old[u] = (mst[h], lst[h], acc[:, :, at[u]].reshape(2 * BLK, HD))
            parts = []
            for load, masks in keys:
                sc = lax.dot_general(
                    qh,
                    load(h, 0),
                    (((1,), (1,)), ((), ())),
                    preferred_element_type=jnp.float32,
                )
                for k in range(sc.shape[1] // HD):
                    part = sc[:, k * HD : (k + 1) * HD]
                    if masks is not None:
                        part = jnp.concatenate(
                            [part[:BLK] + masks[k][0], part[BLK:] + masks[k][1]], axis=0
                        )
                    parts.append(part)
            scores[u] = parts
        for work in beside:
            work()
        for u in range(UH):
            peak = scores[u][0]
            for part in scores[u][1:]:
                peak = jnp.maximum(peak, part)
            peak = jnp.max(peak, axis=-1, keepdims=True)
            if first:
                new[u] = jnp.broadcast_to(peak, (2 * BLK, HD))
            else:
                new[u] = jnp.maximum(old[u][0], peak)
        for work in ():
            work()
        for u in range(UH):
            ps = [jnp.exp2(part - new[u]) for part in scores[u]]
            pv, k = None, 0
            for load, _ in keys:
                v = load(i * UH + u, 1)
                n = v.shape[0] // HD
                p = ps[k] if n == 1 else jnp.concatenate(ps[k : k + n], axis=1)
                k += n
                v = jnp.concatenate([v, jnp.ones_like(v)], axis=1)
                y = jnp.dot(
                    p.astype(jnp.bfloat16), v, preferred_element_type=jnp.float32
                )
                pv = y if pv is None else pv + y
            pv, total = pv[:, :HD], pv[:, HD:]
            if not first:
                alpha = jnp.exp2(old[u][0] - new[u])
                total = old[u][1] * alpha + total
                pv = old[u][2] * alpha + pv
            done[u] = (total, pv)
        for u in range(UH):
            total, pv = done[u]
            if last:
                y = (pv / total).astype(jnp.bfloat16)
                att[:, :, at[u]] = y.reshape(2, BLK, HD)
            else:
                h = i * UH + u
                mst[h] = new[u]
                lst[h] = total
                acc[:, :, at[u]] = pv.reshape(2, BLK, HD)

    def attend(keys, first, last, before=None):
        def body(i, carry):
            if before is not None:
                before(i)
            heads(i, keys, first, last)
            return carry

        lax.fori_loop(0, HEADS // UH, body, 0)

    def cols_of(h, which, base):
        return pl.ds(aligned(base + which * D + h * HD), HD)

    def own_keys(h, which):
        return qkv[:, :, cols_of(h, which, D)].reshape(2 * BLK, HD)

    def near_keys(h, which):
        return kvn[:, :, cols_of(h, which, 0)].reshape(2 * BLK, HD)

    def far_keys(i):
        return lambda h, which: kvf[i, :, cols_of(h, which, 0)]

    def layer(l, src, emit):
        n = CH if l == 0 else SH
        for c in range(n):
            rows = pl.ds(c * (BLK // n), BLK // n)
            if l == 0 and c < 2:
                x_in[c].wait()
            if l == 1:
                shift(c).wait_recv()
            for r in range(2):
                mown[r, rows] = normed(src[r, rows])
            select(l, (0, 1), rows)
            if l == 0 and c == 0:
                peers = 2 + has_up.astype(jnp.int32) + has_down.astype(jnp.int32)
                pl.semaphore_wait(barrier, peers)
            for f in (0, 1):

                @pl.when(sends(f))
                def _():
                    flow(l, f, c, n).start()

        select(l, (2, 3), pl.ds(0, BLK))
        for f in (2, 3):

            @pl.when(sends(f))
            def _():
                for c in range(CH):
                    flow(l, f, c, CH).start()


        if l == 0:
            for f in (0, 1, 4, 5):

                @pl.when(jnp.logical_not(receives(f)))
                def _():
                    for l in range(2):
                        rcv[l, f] = jnp.zeros((BLK, D), jnp.bfloat16)

            for d in (-1, 1, -2, 2):
                bias[d] = [bias_of(r, d) for r in range(2)]
            lane = lax.broadcasted_iota(jnp.int32, (1, HD), 1)
            for r in range(2):
                far.append(jnp.where(lane < BLK // 2, bias[-2][r], bias[2][r]))
            for cp in w_in[:3]:
                cp.wait()

        def put_own(cols, y):
            qkv[:, :, cols] = y.reshape(2, BLK, TN)

        project(lambda: mown[...].reshape(2 * BLK, D), 0, 3, put_own, True)

        for f in (0, 1):

            @pl.when(receives(f))
            def _():
                for c in range(n):
                    flow(l, f, c, n).wait_recv()

        def put_near(cols, y):
            kvn[:, :, cols] = y.reshape(2, BLK, TN)

        project(lambda: rcv[l, 0:2].reshape(2 * BLK, D), D, 2, put_near)


        def relay(c):
            @pl.when(interior)
            def _():
                for f in (2, 3):
                    flow(l, f, c, CH).wait_recv()
                    flow(l, f + 2, c, CH).start()

        attend([(own_keys, None), (near_keys, (bias[-1], bias[1]))], True, False, relay)
        for c in range(HEADS // UH, CH):
            relay(c)

        half = BLK // 2
        for i in range(2):
            rows = pl.ds(i * half, half)
            for f in (4, 5):

                @pl.when(receives(f))
                def _():
                    for c in range(i * CH // 2, (i + 1) * CH // 2):
                        flow(l, f, c, CH).wait_recv()

            groups = HEADS // UH
            wide = UH * HD

            def keys_of(first):
                def work():
                    y = jnp.dot(
                        rcv[l, 4:6, rows].reshape(2 * half, D),
                        wqkv[:, pl.ds(D + first, wide)],
                        preferred_element_type=jnp.float32,
                    )
                    kvf[i, :, pl.ds(first, wide)] = y.astype(jnp.bfloat16)

                return work

            pending = [[keys_of(j * wide), keys_of(D + j * wide)] for j in range(groups)]
            for work in pending[0]:
                work()
            for j in range(groups):
                beside = pending[j + 1] if j + 1 < groups else []
                heads(j, [(far_keys(i), (far,))], False, i == 1, beside)

        if l == 0:
            w_in[3].wait()
        for j in range(D // TN):
            cols = pl.ds(j * TN, TN)
            y = jnp.dot(
                att[...].reshape(2 * BLK, D),
                wout[:, cols],
                preferred_element_type=jnp.float32,
            )
            res = src[:, :, cols].astype(jnp.float32).reshape(2 * BLK, TN)
            res = res + mod[2, :, cols] * y
            emit(cols, res.astype(jnp.bfloat16).reshape(2, BLK, TN))

    def emit_first(cols, y):
        x1[:, :, cols] = y

    def emit_second(cols, y):
        out_ref[:, :, cols] = y

    layer(0, xbuf, emit_first)
    for c in range(SH):
        shift(c).start()
    layer(1, xin, emit_second)

    for c in range(SH):
        shift(c).wait_send()
    for f in range(6):

        @pl.when(sends(f))
        def _():
            for l in range(2):
                n = SH if l == 1 and f < 2 else CH
                for c in range(n):
                    flow(l, f, c, n).wait_send()


def on_device(sections, seqs, activations, qkv_weight, out_weight, modulation, key_blocks, block_counts):
    bf16, f32 = jnp.bfloat16, jnp.float32
    dma = pltpu.SemaphoreType.DMA
    out = pl.pallas_call(
        functools.partial(kernel, sections, seqs),
        out_shape=pltpu.VMEM((2, BLK, D), bf16),
        in_specs=[
            pl.BlockSpec(memory_space=pltpu.SMEM),
            pl.BlockSpec(memory_space=pltpu.SMEM),
            pl.BlockSpec(memory_space=pltpu.HBM),
            pl.BlockSpec(memory_space=pltpu.HBM),
            pl.BlockSpec(memory_space=pltpu.HBM),
            pl.BlockSpec(memory_space=pltpu.VMEM),
        ],
        out_specs=pl.BlockSpec(memory_space=pltpu.VMEM),
        scratch_shapes=[
            pltpu.VMEM((2, BLK, D), bf16),
            pltpu.VMEM((2, BLK, D), bf16),
            pltpu.VMEM((2, BLK, D), bf16),
            pltpu.VMEM((2, 4, BLK, D), bf16),
            pltpu.VMEM((2, 6, BLK, D), bf16),
            pltpu.VMEM((D, 3 * D), bf16),
            pltpu.VMEM((D, D), bf16),
            pltpu.VMEM((2, BLK, D), bf16),
            pltpu.VMEM((2, BLK, 3 * D), bf16),
            pltpu.VMEM((2, BLK, 2 * D), bf16),
            pltpu.VMEM((2, BLK, 2 * D), bf16),
            pltpu.VMEM((2, BLK, D), f32),
            pltpu.VMEM((HEADS, 2 * BLK, HD), f32),
            pltpu.VMEM((HEADS, 2 * BLK, HD), f32),
            pltpu.VMEM((2, BLK, D), bf16),
            dma((6,)),
            dma((2, 6, SH)),
            dma((2, 6, SH)),
            dma((SH,)),
            dma((SH,)),
        ],
        compiler_params=pltpu.CompilerParams(
            collective_id=0, has_side_effects=True, vmem_limit_bytes=62 * 1024 * 1024
        ),
        name="two_layers",
    )(
        key_blocks.T,
        block_counts,
        activations.reshape(2, BLK, D),
        qkv_weight[0],
        out_weight[0],
        modulation.transpose(1, 0, 2),
    )
    return out.reshape(1, 2 * BLK, D)


def solution(mesh):
    return jax.shard_map(
        functools.partial(on_device, mesh.shape["section"], mesh.shape["seq"]),
        mesh=mesh,
        in_specs=(
            P("section", "seq", None),
            P("section", None, None),
            P("section", None, None),
            P("section", None, None),
            P(),
            P(),
        ),
        out_specs=P("section", "seq", None),
        check_vma=False,
    )
```
